32 devices in a mesh: parts: 2 (over y), step: 4 (over z), frame: 2 (over x), head: 2 (over core).
Axes of the slice: x: 2, y: 2, z: 4, core: 2. Of those that a mesh axis runs over, the one named last changes fastest.
Arguments:
- start_noise: float32 [32, 256], P('parts', 'frame'), parts along dimension 0, may hold values from -6 to 6
- position: bfloat16 [256, 1152], P('frame'), may hold values from -6 to 6
- time_table: bfloat16 [128, 1152], replicated, may hold values from -6 to 6
- time_index: int32 [4], P('step'), may hold values from 0 to 127
- sched_index: int32 [4], P('step'), may hold values from 0 to 127
- coef_keep: float32 [128], replicated, may hold values from -0.06 to -0.01
- coef_noise: float32 [128], replicated, may hold values from 0.03 to 0.12
- w_in: bfloat16 [16, 1152], replicated, may hold values from -1.5 to 1.5
- norm_gain: float32 [1152], replicated, may hold values from 0.5 to 1.5
- w_qkv: bfloat16 [1152, 3, 1152], P('step', None, 'head'), may hold values from -4 to 4
- w_proj: bfloat16 [1152, 1152], P('step', 'head'), may hold values from -0.1875 to 0.1875
- w_final: bfloat16 [16, 1152], replicated, may hold values from -0.1875 to 0.1875
Outputs:
- trajectory: float32 [4, 32, 256], P('step', 'parts', 'frame'), parts along dimension 1
- residual_norms: float32 [8], P('parts'), parts along dimension 0
The draws below stay inside these ranges and needn't reach their ends.
There are 2 independent parts, one for each index of `parts`. The reference program is written for one: setup_inputs(seed, part) draws one part's arguments, and reference() takes and returns one part's arrays. A program takes and returns all parts, laid end to end along the dimension named above; an argument that names none is the same for every part. Nothing has to cross between parts.
All inputs are finite; a program needn't handle non-finite values.
Results may differ from the reference program's by a relative error of at most 0.0044.
Values may be sent and summed in bfloat16 or wider, within the bound.
A program may use at most 64 MiB of HBM per device.

```python
import math
import jax
import jax.numpy as jnp
from jax import lax

D = 1152
HEADS = 16
HDIM = 72
HQ = 1152
LAT_C = 16
NTOK = 256
STEPS = 4
SCHED = 128
ITERS = 4


def draw_w_qkv(key, part):
    base_key = jax.random.fold_in(jax.random.fold_in(key, 17), 0)
    base = jnp.clip(jax.random.normal(base_key, (D, 3, HQ), jnp.float32), -6.0, 6.0) * D ** (-0.5)
    return base.astype(jnp.bfloat16)


def place_ends(drawn, key, least, top_value):
    dims = drawn.shape
    place = [jax.random.randint(jax.random.fold_in(key, axis), (), 0, dims[axis]) for axis in range(len(dims))]
    drawn = drawn.at[tuple(place)].set(least)
    longest = dims.index(max(dims))
    place[longest] = (place[longest] + 1) % dims[longest]
    return drawn.at[tuple(place)].set(top_value)


def level_of(stream_key, shape, pieces, least, top_value):
    loudness, own = 1.0, jax.random.fold_in(stream_key, 6)
    for axis_at, parts in pieces:
        draws = jnp.exp(jax.random.uniform(jax.random.fold_in(own, axis_at), (parts,), jnp.float32, least / len(pieces), top_value / len(pieces)))
        loudness = loudness * jnp.repeat(draws, shape[axis_at] // parts).reshape([-1 if axis == axis_at else 1 for axis in range(len(shape))])
    return loudness


def scatter_about(own_key, dims, spread, most, shards=(), kind=jnp.bfloat16):
    array = spread * jax.random.normal(own_key, dims, jnp.float32)
    if shards:
        array = array * level_of(own_key, dims, shards, -0.22, 0.18)
    return jnp.clip(array, -most, most).astype(kind)


def setup_inputs(seed: int = 0, part: int = 0) -> dict:
    keys = jax.random.split(jax.random.key(seed), 13)
    part_keys = jax.random.split(jax.random.fold_in(keys[12], part), 13)
    start_noise = scatter_about(part_keys[0], (LAT_C, NTOK), 1.0, 6.0, ((1, 2),), jnp.float32)
    position = scatter_about(keys[1], (NTOK, D), 1.0, 6.0, ((0, 2),))
    time_table = scatter_about(keys[2], (SCHED, D), 1.0, 6.0)
    time_index = place_ends(jax.random.randint(keys[3], (STEPS,), 0, SCHED), jax.random.fold_in(keys[3], 1), 0, SCHED - 1).astype(jnp.int32)
    sched_index = place_ends(jax.random.randint(keys[4], (STEPS,), 0, SCHED), jax.random.fold_in(keys[4], 1), 0, SCHED - 1).astype(jnp.int32)
    coef_keep = jnp.clip(jax.random.uniform(keys[5], (SCHED,), jnp.float32, -0.06, -0.01), -0.06, -0.01)
    coef_noise = jnp.clip(jax.random.uniform(keys[6], (SCHED,), jnp.float32, 0.03, 0.12), 0.03, 0.12)
    w_in = scatter_about(keys[7], (LAT_C, D), LAT_C ** -0.5, 1.5)
    norm_gain = jnp.clip(1.0 + 0.1 * jax.random.normal(keys[8], (D,), jnp.float32), 0.5, 1.5)
    w_qkv = draw_w_qkv(jax.random.fold_in(keys[12], 71), part)
    w_proj = scatter_about(keys[10], (D, HQ), HQ ** -0.5, 0.1875, ((0, 4), (1, 2)))
    w_final = scatter_about(keys[11], (LAT_C, D), D ** -0.5, 0.1875)
    return dict(start_noise=start_noise, position=position, time_table=time_table, time_index=time_index, sched_index=sched_index, coef_keep=coef_keep, coef_noise=coef_noise, w_in=w_in, norm_gain=norm_gain, w_qkv=w_qkv, w_proj=w_proj, w_final=w_final)


def one_head(packed):
    queries, keys_part, values_part = packed
    scores = jnp.dot(queries, keys_part.T, preferred_element_type=jnp.float32) / math.sqrt(HDIM)
    top_score = lax.optimization_barrier(jnp.max(scores, axis=1, keepdims=True))
    weights_exp = jnp.exp(scores - top_score)
    totals = lax.optimization_barrier(jnp.sum(weights_exp, axis=1, keepdims=True))
    attended = jnp.dot(weights_exp.astype(jnp.bfloat16), values_part, preferred_element_type=jnp.float32)
    return (attended / totals).astype(jnp.bfloat16)

def denoise(latent, time_row, position, w_in, norm_gain, w_qkv, w_proj, w_final):
    latent_bf = latent.astype(jnp.bfloat16)
    hidden = jnp.dot(latent_bf.T, w_in, preferred_element_type=jnp.float32) + position.astype(jnp.float32) + time_row[None, :]
    normed = (hidden * lax.rsqrt(lax.optimization_barrier(jnp.mean(hidden * hidden, axis=1, keepdims=True)) + 1e-06) * norm_gain[None, :]).astype(jnp.bfloat16)
    projected = jnp.einsum('nd,dkq->nkq', normed.astype(jnp.float32), w_qkv.astype(jnp.float32)).astype(jnp.bfloat16)
    token_count = projected.shape[0]
    split_heads = projected.reshape(token_count, 3, HEADS, HDIM).transpose(1, 2, 0, 3)
    attended = lax.map(one_head, (split_heads[0], split_heads[1], split_heads[2]))
    attended = attended.transpose(1, 0, 2).reshape(token_count, HEADS * HDIM)
    branch = jnp.dot(attended, w_proj.T, preferred_element_type=jnp.float32)
    joined = (hidden + branch).astype(jnp.bfloat16)
    return jnp.dot(w_final, joined.T, preferred_element_type=jnp.float32)

def reference(start_noise, position, time_table, time_index, sched_index, coef_keep, coef_noise, w_in, norm_gain, w_qkv, w_proj, w_final):
    time_embed = time_table[time_index].astype(jnp.float32)
    keep_rate = coef_keep[sched_index]
    noise_rate = coef_noise[sched_index]
    states = jnp.broadcast_to(start_noise[None], (STEPS,) + start_noise.shape)

    def one_step(packed):
        return denoise(packed[0], packed[1], position, w_in, norm_gain, w_qkv, w_proj, w_final)
    residual_list = []
    drift_term = jnp.zeros_like(states)
    for iteration in range(ITERS):
        predicted = lax.map(one_step, (states, time_embed))
        drift_term = keep_rate[:, None, None] * states + noise_rate[:, None, None] * predicted
        running = jnp.cumsum(drift_term, axis=0)
        before = jnp.concatenate([jnp.zeros_like(running[:1]), running[:-1]], axis=0)
        new_states = start_noise[None] + before
        change = new_states - states
        residual_list.append(jnp.sqrt(jnp.mean(change * change) + 1e-06))
        states = new_states
    trajectory = states + drift_term
    return (trajectory, jnp.stack(residual_list))
```

```python
import functools
import math

import jax
import jax.numpy as jnp
from jax import lax
from jax.experimental import pallas as pl
from jax.experimental.pallas import tpu as pltpu
from jax.sharding import PartitionSpec as P

HDIM = 72
ITERS = 4


def entering(value, axis, combine, identity):
    count, here = (lax.axis_size(axis), lax.axis_index(axis))
    everything = lax.all_gather(value, axis)
    start = jnp.broadcast_to(jnp.asarray(identity, value.dtype), value.shape)

    def hop(k, before):
        reached = k < here
        new = combine(before, everything[k])
        return jnp.where(reached, new, before)

    return lax.fori_loop(0, count, hop, start)


def add_terms(first, second):
    return first + second


def local_any(
    start_noise,
    position,
    time_table,
    time_index,
    sched_index,
    coef_keep,
    coef_noise,
    w_in,
    norm_gain,
    w_qkv,
    w_proj,
    w_final,
):
    w_qkv_all, w_proj_all = (
        lax.all_gather(w_qkv, "step", axis=0, tiled=True),
        lax.all_gather(w_proj, "step", axis=0, tiled=True),
    )
    batch_steps = time_index.shape[0]
    row_count = start_noise.shape[1]
    table_rows = time_table.shape[0]
    pick_time = (time_index[:, None] == jnp.arange(table_rows)[None, :]).astype(jnp.bfloat16)
    time_embed = jnp.dot(pick_time, time_table, preferred_element_type=jnp.float32)
    pick_sched = (sched_index[:, None] == jnp.arange(table_rows)[None, :]).astype(jnp.float32)
    keep_rate = jnp.sum(pick_sched * coef_keep[None, :], axis=1)
    noise_rate = jnp.sum(pick_sched * coef_noise[None, :], axis=1)
    heads_local = w_qkv_all.shape[2] // HDIM
    cell_count = (
        batch_steps
        * lax.axis_size("step")
        * start_noise.shape[0]
        * row_count
        * lax.axis_size("frame")
    )
    states = start_noise[None]
    drift_term = jnp.zeros_like(states)
    residual_list = []
    for iteration in range(ITERS):
        latent_bf = states.astype(jnp.bfloat16)
        hidden = (
            jnp.einsum("bcr,cd->brd", latent_bf, w_in, preferred_element_type=jnp.float32)
            + position
            + time_embed[:, None, :]
        )
        normed = (
            hidden * lax.rsqrt(jnp.mean(hidden * hidden, axis=2, keepdims=True) + 1e-06) * norm_gain
        ).astype(jnp.bfloat16)
        projected = jnp.einsum(
            "brd,dkq->brkq", normed, w_qkv_all, preferred_element_type=jnp.float32
        ).astype(jnp.bfloat16)
        queries = projected[:, :, 0].reshape(batch_steps, row_count, heads_local, HDIM)
        score_scale = 1.0 / math.sqrt(HDIM)
        keys_values = projected[:, :, 1:3]
        piece = lax.all_gather(keys_values, "frame", axis=1, tiled=True)
        top_old = jnp.full((batch_steps, heads_local, row_count), -1e30, jnp.float32)
        piece_rows = piece.shape[1]
        keys_blk = piece[:, :, 0].reshape(batch_steps, piece_rows, heads_local, HDIM)
        values_blk = piece[:, :, 1].reshape(batch_steps, piece_rows, heads_local, HDIM)
        scores = (
            jnp.einsum("bqhe,bkhe->bhqk", queries, keys_blk, preferred_element_type=jnp.float32)
            * score_scale
        )
        top_new = jnp.maximum(top_old, jnp.max(scores, axis=3))
        weights_exp = jnp.exp(scores - top_new[:, :, :, None])
        total_new = jnp.sum(weights_exp, axis=3)
        update = jnp.einsum(
            "bhqk,bkhe->bqhe",
            weights_exp.astype(jnp.bfloat16),
            values_blk,
            preferred_element_type=jnp.float32,
        )
        accum = update
        top_final, total_final, accum = (top_new, total_new, accum)
        attended = accum / jnp.transpose(total_final, (0, 2, 1))[:, :, :, None]
        attn_mixed = attended.reshape(batch_steps, row_count, heads_local * HDIM).astype(
            jnp.bfloat16
        )
        partial_value = jnp.einsum(
            "brq,dq->brd", attn_mixed, w_proj_all, preferred_element_type=jnp.float32
        )
        head_total = lax.psum(partial_value, "head")
        joined = (hidden + head_total).astype(jnp.bfloat16)
        predicted = jnp.einsum("cd,brd->bcr", w_final, joined, preferred_element_type=jnp.float32)
        drift_term = keep_rate[:, None, None] * states + noise_rate[:, None, None] * predicted
        local_incl = jnp.cumsum(drift_term, axis=0)
        local_total = local_incl[-1]
        earlier = entering(local_total, "step", add_terms, jnp.zeros_like(local_total))
        before = earlier[None] + (local_incl - drift_term)
        new_states = start_noise[None] + before
        change = new_states - states
        square_sum = jnp.sum(change * change)
        summed = lax.psum(square_sum, ("step", "frame"))
        residual_list.append(jnp.sqrt(summed / cell_count + 1e-06))
        states = new_states
    residual_norms = jnp.stack(residual_list)
    trajectory = states + drift_term
    return (trajectory, residual_norms)


MESH = pl.DeviceIdType.MESH
F32 = jnp.float32
BF16 = jnp.bfloat16


def dot(a, b, ca=1, cb=0):
    return lax.dot_general(a, b, (((ca,), (cb,)), ((), ())), preferred_element_type=F32)


def dot_exact(a, b):
    return lax.dot_general(
        a, b, (((1,), (0,)), ((), ())), precision=lax.Precision.HIGHEST, preferred_element_type=F32
    )


def two(a):
    high = a.astype(BF16)
    return high, (a - high.astype(F32)).astype(BF16)


def evals_of(steps):
    return [(i, j) for j in range(steps - 1) for i in range(min(j, ITERS - 1) + 1)] + [
        (min(ITERS, steps) - 1, steps - 1)
    ]


def kernel(
    S,
    F,
    H,
    noise_ref,
    pos_ref,
    table_ref,
    tidx_ref,
    sidx_ref,
    keep_ref,
    coef_ref,
    win_ref,
    gain_ref,
    wsend_ref,
    msend_ref,
    wfin_ref,
    traj_ref,
    res_ref,
    w_buf,
    m_buf,
    pos_buf,
    noise_buf,
    meta_buf,
    base_buf,
    plane_buf,
    line_buf,
    ssem,
    rsem,
):
    s, f, h = (lax.axis_index(a) for a in ("step", "frame", "head"))
    PL = F * H
    q_me = f * H + h
    C, rows = noise_ref.shape
    D = pos_ref.shape[1]
    N = rows * F
    pad = wsend_ref.shape[2]
    lanes = table_ref.shape[0]

    def step_peer(d):
        return {"step": lax.rem(s + d, S)}

    def plane_peer(d):
        t = lax.rem(q_me + d, PL)
        return {"frame": t // H, "head": lax.rem(t, H)}

    def frame_peer(d):
        return {"frame": lax.rem(f + d, F)}

    barrier = pltpu.get_barrier_semaphore()
    for d in range(1, S):
        pl.semaphore_signal(barrier, inc=1, device_id=step_peer(d), device_id_type=MESH)
    for d in range(1, PL):
        pl.semaphore_signal(barrier, inc=1, device_id=plane_peer(d), device_id_type=MESH)

    row_id = lax.broadcasted_iota(jnp.int32, (8, lanes), 0)
    lane_id = lax.broadcasted_iota(jnp.int32, (1, lanes), 1)
    hot_t = jnp.where(lane_id == tidx_ref[0], 1.0, 0.0)
    hot_s = lane_id == sidx_ref[0]
    keep = jnp.sum(jnp.where(hot_s, keep_ref[...], 0.0), axis=1, keepdims=True)
    coef = jnp.sum(jnp.where(hot_s, coef_ref[...], 0.0), axis=1, keepdims=True)
    meta_buf[s] = jnp.where(row_id == 0, hot_t, jnp.where(row_id == 1, keep, coef))
    w_buf[s] = wsend_ref[s]
    m_buf[s] = msend_ref[s]
    pos_buf[f] = pos_ref[...]
    noise_buf[f] = noise_ref[...]
    pl.semaphore_wait(barrier, S - 1 + PL - 1)

    count = [0]
    started = []

    def send(src, dst, peer):
        k = count[0]
        count[0] += 1
        copy = pltpu.make_async_remote_copy(
            src_ref=src,
            dst_ref=dst,
            send_sem=ssem.at[k],
            recv_sem=rsem.at[k],
            device_id=peer,
            device_id_type=MESH,
        )
        copy.start()
        started.append(copy)
        return copy

    order = sorted(range(1, S), key=lambda d: abs(d - S / 2))
    early = [send(meta_buf.at[s], meta_buf.at[s], step_peer(d)) for d in order]
    early += [send(noise_ref, noise_buf.at[f], frame_peer(d)) for d in range(1, F)]
    early += [send(pos_ref, pos_buf.at[f], frame_peer(d)) for d in range(1, F)]
    late = [
        send(wsend_ref.at[lax.rem(s + d, S)], w_buf.at[s], step_peer(d)) for d in order
    ]
    late += [
        send(msend_ref.at[lax.rem(s + d, S)], m_buf.at[s], step_peer(d)) for d in order
    ]
    for copy in early:
        copy.wait_recv()

    pos = pos_buf[...].reshape(N, D)
    start = jnp.concatenate([noise_buf[i] for i in range(F)], axis=1)
    metas = [meta_buf[j] for j in range(S)]
    hot = jnp.concatenate(
        [m[0:1] for m in metas] + [jnp.zeros((8 - S, lanes), F32)], axis=0
    ).astype(BF16)
    keeps = [jnp.concatenate([m[1:2, :rows]] * F, axis=1) for m in metas]
    coefs = [jnp.concatenate([m[2:3, :rows]] * F, axis=1) for m in metas]
    temb = dot(hot, table_ref[...])
    temb_b = temb.astype(BF16)
    gain = gain_ref[...]
    w_in = win_ref[...]
    posf = pos.astype(F32)
    p_hi, p_lo = two(posf * gain)
    side = jnp.concatenate(
        [w_in.astype(F32), temb, jnp.zeros((128 - C - 8, D), F32)], axis=0
    )
    q_hi, q_lo = two(side * gain)
    left = jnp.concatenate([p_hi, p_lo, q_hi, q_lo], axis=0)
    ends = jnp.concatenate([w_in, wfin_ref[...]], axis=0)
    ends_pos = dot(ends, pos, 1, 1)
    ends_t = dot(ends, temb_b, 1, 1)
    ends_in = dot(ends, w_in, 1, 1)
    sq_hi, sq_lo = two(posf * posf)
    ones = jnp.ones((8, D), BF16)
    norm_p = dot(ones, sq_hi, 1, 1) + dot(ones, sq_lo, 1, 1)
    cross = dot(temb_b, pos, 1, 1)
    norm_t = jnp.sum(temb * temb, axis=1, keepdims=True)
    norms = [norm_p[0:1] + 2.0 * cross[j : j + 1] + norm_t[j : j + 1] for j in range(S)]

    for copy in late:
        copy.wait_recv()

    wide = dot(left, w_buf[...].reshape(D, pad))
    by_pos = jnp.transpose(wide[0:N] + wide[N : 2 * N])
    by_side = jnp.transpose(wide[2 * N : 2 * N + 128] + wide[2 * N + 128 :])
    mix = m_buf[0]
    for j in range(1, S):
        mix = mix + m_buf[j]
    scale = 1.4426950408889634 / math.sqrt(HDIM)

    def table_of(t):
        return jnp.concatenate(
            [
                t[0:HDIM] * scale,
                t[HDIM : 2 * HDIM],
                dot_exact(mix, t[2 * HDIM : 3 * HDIM]),
            ],
            axis=0,
        )

    tab_pos, tab_side = table_of(by_pos), table_of(by_side)
    big_hi, big_lo = two(jnp.concatenate([tab_side[:, 0:C], ends_in], axis=0))
    for j in range(S):
        base_buf[j] = jnp.concatenate(
            [
                tab_pos + tab_side[:, C + j : C + j + 1],
                2.0 * (ends_pos[0:C] + ends_t[0:C, j : j + 1]),
                ends_pos[C : 2 * C] + ends_t[C : 2 * C, j : j + 1],
            ],
            axis=0,
        )
    QK = 2 * HDIM

    def partial(x, j):
        xb = x.astype(BF16)
        lin = dot(big_hi, xb) + dot(big_lo, xb) + base_buf[j]
        square = jnp.sum(xb.astype(F32) * lin[QK + C : QK + 2 * C], axis=0, keepdims=True)
        square = jnp.maximum(square + norms[j], 0.0)
        r = lax.rsqrt(square * (1.0 / D) + 1e-06)
        q = (lin[0:HDIM] * r).astype(BF16)
        k = (lin[HDIM:QK] * r).astype(BF16)
        v_hi, v_lo = two(lin[QK : QK + C] * r)
        scores = dot(k, q, 0, 0)
        e = jnp.exp2(scores - jnp.max(scores, axis=0, keepdims=True)).astype(BF16)
        o = dot(jnp.concatenate([v_hi, v_lo, jnp.ones((C, N), BF16)], axis=0), e)
        out = (o[0:C] + o[C : 2 * C]) / o[2 * C : 2 * C + 1]
        return out, lin[QK + 2 * C : QK + 3 * C]

    keys = evals_of(S)
    state, local_eps, drift, flying = {}, {}, {}, {}

    def launch(key):
        i, j = key
        n = keys.index(key)
        x = start
        for m in range(j if i else 0):
            x = x + drift[(min(i - 1, m), m)]
        state[key] = x
        part, local_eps[key] = partial(x, j)
        plane_buf[n, q_me] = part
        slot = plane_buf.at[n, q_me]
        flying[key] = [send(slot, slot, plane_peer(d)) for d in range(1, PL)]

    def relay(key):
        n = keys.index(key)
        for copy in flying[key]:
            copy.wait_recv()
        total = plane_buf[n, 0]
        for i in range(1, PL):
            total = total + plane_buf[n, i]
        line_buf[n, s] = total
        slot = line_buf.at[n, s]
        flying[key] = [send(slot, slot, step_peer(d)) for d in order]

    def land(key):
        n, j = keys.index(key), key[1]
        for copy in flying[key]:
            copy.wait_recv()
        total = local_eps[key]
        for i in range(S):
            total = total + line_buf[n, i]
        drift[key] = keeps[j] * state[key] + coefs[j] * total

    for act, key in PLAN:
        {"launch": launch, "relay": relay, "land": land}[act](key)

    old = [start] * S
    norms_out = []
    for it in range(ITERS):
        new, run = [], start
        for j in range(S):
            new.append(run)
            if j < S - 1:
                run = run + drift[(min(it, j), j)]
        square = jnp.zeros((1, 1), F32)
        for j in range(S):
            change = new[j] - old[j]
            square = square + jnp.sum(
                jnp.sum(change * change, axis=0, keepdims=True), axis=1, keepdims=True
            )
        norms_out.append(jnp.sqrt(square / (S * C * N) + 1e-06))
        old = new
    lane = lax.broadcasted_iota(jnp.int32, res_ref.shape, 1)
    res = jnp.zeros(res_ref.shape, F32)
    for it in range(ITERS):
        res = jnp.where(lane == it, norms_out[it], res)
    res_ref[...] = res
    mine = jnp.zeros((C, N), F32)
    for j in range(S):
        mine = jnp.where(s == j, old[j] + drift[(min(ITERS - 1, j), j)], mine)
    half = mine[:, 0:rows]
    for i in range(1, F):
        half = jnp.where(f == i, mine[:, i * rows : (i + 1) * rows], half)
    traj_ref[0] = half
    for copy in started:
        copy.wait_send()


PLAN = (
    ("launch", (0, 0)),
    ("launch", (0, 1)),
    ("relay", (0, 0)),
    ("launch", (0, 2)),
    ("relay", (0, 1)),
    ("land", (0, 0)),
    ("launch", (1, 1)),
    ("relay", (0, 2)),
    ("relay", (1, 1)),
    ("land", (0, 1)),
    ("launch", (1, 2)),
    ("land", (1, 1)),
    ("launch", (2, 2)),
    ("relay", (1, 2)),
    ("relay", (2, 2)),
    ("land", (0, 2)),
    ("land", (1, 2)),
    ("land", (2, 2)),
    ("launch", (3, 3)),
    ("relay", (3, 3)),
    ("land", (3, 3)),
)


def local_heads(
    start_noise,
    position,
    time_table,
    time_index,
    sched_index,
    coef_keep,
    coef_noise,
    w_in,
    norm_gain,
    w_qkv,
    w_proj,
    w_final,
):
    S, F, H = (lax.axis_size(a) for a in ("step", "frame", "head"))
    s, f = lax.axis_index("step"), lax.axis_index("frame")
    R = w_qkv.shape[0]
    C, rows = start_noise.shape
    D = position.shape[1]
    N = rows * F
    PL = F * H
    wq = w_qkv.reshape(R, 3, S, F, HDIM)
    wq = lax.dynamic_index_in_dim(wq, f, axis=3, keepdims=False)
    wq = jnp.transpose(wq, (2, 0, 1, 3)).reshape(S, R, 3 * HDIM)
    pad = -(-3 * HDIM // 128) * 128
    wq = jnp.pad(wq, ((0, 0), (0, 0), (0, pad - 3 * HDIM)))
    wp = lax.dynamic_index_in_dim(w_proj.reshape(R, S, F, HDIM), f, axis=2, keepdims=False)
    wf = lax.dynamic_slice_in_dim(w_final, s * R, R, axis=1)
    mix = jnp.einsum("cr,rsk->sck", wf, wp, preferred_element_type=F32)
    n_evals = len(evals_of(S))
    n_sems = 3 * (S - 1) + 2 * (F - 1) + n_evals * (PL - 1 + S - 1)
    vmem = pl.BlockSpec(memory_space=pltpu.VMEM)
    smem = pl.BlockSpec(memory_space=pltpu.SMEM)
    traj, res = pl.pallas_call(
        functools.partial(kernel, S, F, H),
        out_shape=(
            jax.ShapeDtypeStruct((1, C, rows), F32),
            jax.ShapeDtypeStruct((1, ITERS), F32),
        ),
        in_specs=[vmem, vmem, vmem, smem, smem] + [vmem] * 7,
        out_specs=(vmem, vmem),
        scratch_shapes=[
            pltpu.VMEM((S, R, pad), BF16),
            pltpu.VMEM((S, C, HDIM), F32),
            pltpu.VMEM((F, rows, D), BF16),
            pltpu.VMEM((F, C, rows), F32),
            pltpu.VMEM((S, 8, time_table.shape[0]), F32),
            pltpu.VMEM((S, 2 * HDIM + 3 * C, N), F32),
            pltpu.VMEM((n_evals, PL, C, N), F32),
            pltpu.VMEM((n_evals, S, C, N), F32),
            pltpu.SemaphoreType.DMA((n_sems,)),
            pltpu.SemaphoreType.DMA((n_sems,)),
        ],
        compiler_params=pltpu.CompilerParams(
            collective_id=0, has_side_effects=True, vmem_limit_bytes=48 * 1024 * 1024
        ),
    )(
        start_noise,
        position,
        time_table,
        time_index,
        sched_index,
        coef_keep[None],
        coef_noise[None],
        w_in,
        norm_gain[None],
        wq,
        mix,
        w_final,
    )
    return traj, res.reshape(ITERS)


def one_head_each(mesh, start_noise, time_index, w_qkv, time_table):
    S, F, H = (mesh.shape[a] for a in ("step", "frame", "head"))
    return (
        S == ITERS
        and time_index.shape[0] == S
        and w_qkv.shape[2] == S * F * H * HDIM
        and w_qkv.shape[0] % (16 * S) == 0
        and start_noise.shape[1] % (128 * F) == 0
        and start_noise.shape[1] // F <= time_table.shape[0]
        and time_table.shape[0] % 128 == 0
    )


def solution(mesh):
    def call(*args):
        fits = one_head_each(mesh, args[0], args[3], args[9], args[2])
        return jax.shard_map(
            local_heads if fits else local_any,
            mesh=mesh,
            in_specs=(
                P("parts", "frame"),
                P("frame", None),
                P(),
                P("step"),
                P("step"),
                P(),
                P(),
                P(),
                P(),
                P("step", None, "head"),
                P("step", "head"),
                P(),
            ),
            out_specs=(P("step", "parts", "frame"), P("parts")),
            check_vma=False,
        )(*args)

    return call
```

```python
import functools
import math

import jax
import jax.numpy as jnp
from jax import lax
from jax.experimental import pallas as pl
from jax.experimental.pallas import tpu as pltpu
from jax.sharding import PartitionSpec as P

HDIM = 72
ITERS = 4


def entering(value, axis, combine, identity):
    count, here = (lax.axis_size(axis), lax.axis_index(axis))
    everything = lax.all_gather(value, axis)
    start = jnp.broadcast_to(jnp.asarray(identity, value.dtype), value.shape)

    def hop(k, before):
        reached = k < here
        new = combine(before, everything[k])
        return jnp.where(reached, new, before)

    return lax.fori_loop(0, count, hop, start)


def add_terms(first, second):
    return first + second


def local_any(
    start_noise,
    position,
    time_table,
    time_index,
    sched_index,
    coef_keep,
    coef_noise,
    w_in,
    norm_gain,
    w_qkv,
    w_proj,
    w_final,
):
    w_qkv_all, w_proj_all = (
        lax.all_gather(w_qkv, "step", axis=0, tiled=True),
        lax.all_gather(w_proj, "step", axis=0, tiled=True),
    )
    batch_steps = time_index.shape[0]
    row_count = start_noise.shape[1]
    table_rows = time_table.shape[0]
    pick_time = (time_index[:, None] == jnp.arange(table_rows)[None, :]).astype(jnp.bfloat16)
    time_embed = jnp.dot(pick_time, time_table, preferred_element_type=jnp.float32)
    pick_sched = (sched_index[:, None] == jnp.arange(table_rows)[None, :]).astype(jnp.float32)
    keep_rate = jnp.sum(pick_sched * coef_keep[None, :], axis=1)
    noise_rate = jnp.sum(pick_sched * coef_noise[None, :], axis=1)
    heads_local = w_qkv_all.shape[2] // HDIM
    cell_count = (
        batch_steps
        * lax.axis_size("step")
        * start_noise.shape[0]
        * row_count
        * lax.axis_size("frame")
    )
    states = start_noise[None]
    drift_term = jnp.zeros_like(states)
    residual_list = []
    for iteration in range(ITERS):
        latent_bf = states.astype(jnp.bfloat16)
        hidden = (
            jnp.einsum("bcr,cd->brd", latent_bf, w_in, preferred_element_type=jnp.float32)
            + position
            + time_embed[:, None, :]
        )
        normed = (
            hidden * lax.rsqrt(jnp.mean(hidden * hidden, axis=2, keepdims=True) + 1e-06) * norm_gain
        ).astype(jnp.bfloat16)
        projected = jnp.einsum(
            "brd,dkq->brkq", normed, w_qkv_all, preferred_element_type=jnp.float32
        ).astype(jnp.bfloat16)
        queries = projected[:, :, 0].reshape(batch_steps, row_count, heads_local, HDIM)
        score_scale = 1.0 / math.sqrt(HDIM)
        keys_values = projected[:, :, 1:3]
        piece = lax.all_gather(keys_values, "frame", axis=1, tiled=True)
        top_old = jnp.full((batch_steps, heads_local, row_count), -1e30, jnp.float32)
        piece_rows = piece.shape[1]
        keys_blk = piece[:, :, 0].reshape(batch_steps, piece_rows, heads_local, HDIM)
        values_blk = piece[:, :, 1].reshape(batch_steps, piece_rows, heads_local, HDIM)
        scores = (
            jnp.einsum("bqhe,bkhe->bhqk", queries, keys_blk, preferred_element_type=jnp.float32)
            * score_scale
        )
        top_new = jnp.maximum(top_old, jnp.max(scores, axis=3))
        weights_exp = jnp.exp(scores - top_new[:, :, :, None])
        total_new = jnp.sum(weights_exp, axis=3)
        update = jnp.einsum(
            "bhqk,bkhe->bqhe",
            weights_exp.astype(jnp.bfloat16),
            values_blk,
            preferred_element_type=jnp.float32,
        )
        accum = update
        top_final, total_final, accum = (top_new, total_new, accum)
        attended = accum / jnp.transpose(total_final, (0, 2, 1))[:, :, :, None]
        attn_mixed = attended.reshape(batch_steps, row_count, heads_local * HDIM).astype(
            jnp.bfloat16
        )
        partial_value = jnp.einsum(
            "brq,dq->brd", attn_mixed, w_proj_all, preferred_element_type=jnp.float32
        )
        head_total = lax.psum(partial_value, "head")
        joined = (hidden + head_total).astype(jnp.bfloat16)
        predicted = jnp.einsum("cd,brd->bcr", w_final, joined, preferred_element_type=jnp.float32)
        drift_term = keep_rate[:, None, None] * states + noise_rate[:, None, None] * predicted
        local_incl = jnp.cumsum(drift_term, axis=0)
        local_total = local_incl[-1]
        earlier = entering(local_total, "step", add_terms, jnp.zeros_like(local_total))
        before = earlier[None] + (local_incl - drift_term)
        new_states = start_noise[None] + before
        change = new_states - states
        square_sum = jnp.sum(change * change)
        summed = lax.psum(square_sum, ("step", "frame"))
        residual_list.append(jnp.sqrt(summed / cell_count + 1e-06))
        states = new_states
    residual_norms = jnp.stack(residual_list)
    trajectory = states + drift_term
    return (trajectory, residual_norms)


MESH = pl.DeviceIdType.MESH
F32 = jnp.float32
BF16 = jnp.bfloat16


def dot(a, b, ca=1, cb=0):
    return lax.dot_general(a, b, (((ca,), (cb,)), ((), ())), preferred_element_type=F32)


def dot_exact(a, b):
    return lax.dot_general(
        a, b, (((1,), (0,)), ((), ())), precision=lax.Precision.HIGHEST, preferred_element_type=F32
    )


def two(a):
    high = a.astype(BF16)
    return high, (a - high.astype(F32)).astype(BF16)


def evals_of(steps):
    return [(i, j) for j in range(steps - 1) for i in range(min(j, ITERS - 1) + 1)] + [
        (min(ITERS, steps) - 1, steps - 1)
    ]


def kernel(
    S,
    F,
    H,
    noise_hbm,
    pos_hbm,
    table_hbm,
    tidx_ref,
    sidx_ref,
    keep_hbm,
    coef_hbm,
    win_hbm,
    gain_hbm,
    wqkv_hbm,
    wproj_hbm,
    wfin_hbm,
    traj_ref,
    res_ref,
    table_ref,
    keep_ref,
    coef_ref,
    win_ref,
    gain_ref,
    wqkv_ref,
    wproj_ref,
    wfin_ref,
    w_buf,
    m_buf,
    pos_buf,
    noise_buf,
    meta_buf,
    base_buf,
    plane_buf,
    line_buf,
    wsend_ref,
    msend_ref,
    ssem,
    rsem,
):
    s, f, h = (lax.axis_index(a) for a in ("step", "frame", "head"))
    loads = [
        pltpu.make_async_copy(src, dst, ssem.at[ssem.shape[0] - 1 - n])
        for n, (src, dst) in enumerate(
            (
                (pos_hbm, pos_buf.at[f]),
                (noise_hbm, noise_buf.at[f]),
                (keep_hbm, keep_ref),
                (coef_hbm, coef_ref),
                (wqkv_hbm, wqkv_ref),
                (wproj_hbm, wproj_ref),
                (wfin_hbm, wfin_ref),
                (table_hbm, table_ref),
                (win_hbm, win_ref),
                (gain_hbm, gain_ref),
            )
        )
    ]
    for copy in loads:
        copy.start()
    PL = F * H
    q_me = f * H + h
    C, rows = noise_buf.shape[1:]
    D = pos_buf.shape[2]
    N = rows * F
    pad = w_buf.shape[2]
    lanes = table_ref.shape[0]

    def step_peer(d):
        return {"step": lax.rem(s + d, S)}

    def plane_peer(d):
        t = lax.rem(q_me + d, PL)
        return {"frame": t // H, "head": lax.rem(t, H)}

    def frame_peer(d):
        return {"frame": lax.rem(f + d, F)}

    barrier = pltpu.get_barrier_semaphore()
    for d in range(1, S):
        pl.semaphore_signal(barrier, inc=1, device_id=step_peer(d), device_id_type=MESH)
    for d in range(1, PL):
        pl.semaphore_signal(barrier, inc=1, device_id=plane_peer(d), device_id_type=MESH)

    for copy in loads[:4]:
        copy.wait()
    row_id = lax.broadcasted_iota(jnp.int32, (8, lanes), 0)
    lane_id = lax.broadcasted_iota(jnp.int32, (1, lanes), 1)
    hot_t = jnp.where(lane_id == tidx_ref[0], 1.0, 0.0)
    hot_s = lane_id == sidx_ref[0]
    keep = jnp.sum(jnp.where(hot_s, keep_ref[...], 0.0), axis=1, keepdims=True)
    coef = jnp.sum(jnp.where(hot_s, coef_ref[...], 0.0), axis=1, keepdims=True)
    meta_buf[s] = jnp.where(row_id == 0, hot_t, jnp.where(row_id == 1, keep, coef))
    pl.semaphore_wait(barrier, S - 1 + PL - 1)

    count = [0]
    started = []

    def send(src, dst, peer):
        k = count[0]
        count[0] += 1
        copy = pltpu.make_async_remote_copy(
            src_ref=src,
            dst_ref=dst,
            send_sem=ssem.at[k],
            recv_sem=rsem.at[k],
            device_id=peer,
            device_id_type=MESH,
        )
        copy.start()
        started.append(copy)
        return copy

    order = sorted(range(1, S), key=lambda d: abs(d - S / 2))
    early = [send(meta_buf.at[s], meta_buf.at[s], step_peer(d)) for d in order]
    early += [send(noise_buf.at[f], noise_buf.at[f], frame_peer(d)) for d in range(1, F)]
    early += [send(pos_buf.at[f], pos_buf.at[f], frame_peer(d)) for d in range(1, F)]
    for copy in loads[4:7]:
        copy.wait()
    R = wqkv_ref.shape[1]
    for i in range(F):

        @pl.when(f == i)
        def _():
            for t in range(S):
                low = (t * F + i) * HDIM
                parts = [wqkv_ref[p, :, low : low + HDIM] for p in range(3)]
                parts.append(jnp.zeros((R, pad - 3 * HDIM), BF16))
                wsend_ref[t] = jnp.concatenate(parts, axis=1)

    late = [
        send(wsend_ref.at[lax.rem(s + d, S)], w_buf.at[s], step_peer(d)) for d in order
    ]
    rows_of = wfin_ref[:, 0:R].astype(F32)
    for j in range(1, S):
        rows_of = jnp.where(s == j, wfin_ref[:, j * R : (j + 1) * R].astype(F32), rows_of)
    folded = dot(rows_of.astype(BF16), wproj_ref[...])
    for t in range(S):
        picked = folded[:, t * F * HDIM : (t * F + 1) * HDIM]
        for i in range(1, F):
            low = (t * F + i) * HDIM
            picked = jnp.where(f == i, folded[:, low : low + HDIM], picked)
        msend_ref[t] = picked
    late += [
        send(msend_ref.at[lax.rem(s + d, S)], m_buf.at[s], step_peer(d)) for d in order
    ]
    w_buf[s] = wsend_ref[s]
    m_buf[s] = msend_ref[s]
    for copy in loads[7:]:
        copy.wait()
    for copy in early:
        copy.wait_recv()

    pos = pos_buf[...].reshape(N, D)
    start = jnp.concatenate([noise_buf[i] for i in range(F)], axis=1)
    metas = [meta_buf[j] for j in range(S)]
    hot = jnp.concatenate(
        [m[0:1] for m in metas] + [jnp.zeros((8 - S, lanes), F32)], axis=0
    ).astype(BF16)
    keeps = [jnp.concatenate([m[1:2, :rows]] * F, axis=1) for m in metas]
    coefs = [jnp.concatenate([m[2:3, :rows]] * F, axis=1) for m in metas]
    temb = dot(hot, table_ref[...])
    temb_b = temb.astype(BF16)
    gain = gain_ref[...]
    w_in = win_ref[...]
    posf = pos.astype(F32)
    p_hi, p_lo = two(posf * gain)
    side = jnp.concatenate(
        [w_in.astype(F32), temb, jnp.zeros((128 - C - 8, D), F32)], axis=0
    )
    q_hi, q_lo = two(side * gain)
    left = jnp.concatenate([p_hi, p_lo, q_hi, q_lo], axis=0)
    ends = jnp.concatenate([w_in, wfin_ref[...]], axis=0)
    ends_pos = dot(ends, pos, 1, 1)
    ends_t = dot(ends, temb_b, 1, 1)
    ends_in = dot(ends, w_in, 1, 1)
    sq_hi, sq_lo = two(posf * posf)
    ones = jnp.ones((8, D), BF16)
    norm_p = dot(ones, sq_hi, 1, 1) + dot(ones, sq_lo, 1, 1)
    cross = dot(temb_b, pos, 1, 1)
    norm_t = jnp.sum(temb * temb, axis=1, keepdims=True)
    norms = [norm_p[0:1] + 2.0 * cross[j : j + 1] + norm_t[j : j + 1] for j in range(S)]

    for copy in late:
        copy.wait_recv()

    wide = dot(left, w_buf[...].reshape(D, pad))
    by_pos = jnp.transpose(wide[0:N] + wide[N : 2 * N])
    by_side = jnp.transpose(wide[2 * N : 2 * N + 128] + wide[2 * N + 128 :])
    mix = m_buf[0]
    for j in range(1, S):
        mix = mix + m_buf[j]
    scale = 1.4426950408889634 / math.sqrt(HDIM)

    def table_of(t):
        return jnp.concatenate(
            [
                t[0:HDIM] * scale,
                t[HDIM : 2 * HDIM],
                dot_exact(mix, t[2 * HDIM : 3 * HDIM]),
            ],
            axis=0,
        )

    tab_pos, tab_side = table_of(by_pos), table_of(by_side)
    big_hi, big_lo = two(jnp.concatenate([tab_side[:, 0:C], ends_in], axis=0))
    for j in range(S):
        base_buf[j] = jnp.concatenate(
            [
                tab_pos + tab_side[:, C + j : C + j + 1],
                2.0 * (ends_pos[0:C] + ends_t[0:C, j : j + 1]),
                ends_pos[C : 2 * C] + ends_t[C : 2 * C, j : j + 1],
            ],
            axis=0,
        )
    QK = 2 * HDIM

    def partial(x, j):
        xb = x.astype(BF16)
        lin = dot(big_hi, xb) + dot(big_lo, xb) + base_buf[j]
        square = jnp.sum(xb.astype(F32) * lin[QK + C : QK + 2 * C], axis=0, keepdims=True)
        square = jnp.maximum(square + norms[j], 0.0)
        r = lax.rsqrt(square * (1.0 / D) + 1e-06)
        q = (lin[0:HDIM] * r).astype(BF16)
        k = (lin[HDIM:QK] * r).astype(BF16)
        v_hi, v_lo = two(lin[QK : QK + C] * r)
        scores = dot(k, q, 0, 0)
        e = jnp.exp2(scores - jnp.max(scores, axis=0, keepdims=True)).astype(BF16)
        o = dot(jnp.concatenate([v_hi, v_lo, jnp.ones((C, N), BF16)], axis=0), e)
        out = (o[0:C] + o[C : 2 * C]) / o[2 * C : 2 * C + 1]
        return out, lin[QK + 2 * C : QK + 3 * C]

    keys = evals_of(S)
    state, local_eps, drift, flying = {}, {}, {}, {}

    def launch(key):
        i, j = key
        n = keys.index(key)
        x = start
        for m in range(j if i else 0):
            x = x + drift[(min(i - 1, m), m)]
        state[key] = x
        part, local_eps[key] = partial(x, j)
        plane_buf[n, q_me] = part.astype(BF16)
        slot = plane_buf.at[n, q_me]
        flying[key] = [send(slot, slot, plane_peer(d)) for d in range(1, PL)]

    def relay(key):
        n = keys.index(key)
        for copy in flying[key]:
            copy.wait_recv()
        total = plane_buf[n, 0].astype(F32)
        for i in range(1, PL):
            total = total + plane_buf[n, i].astype(F32)
        line_buf[n, s] = total.astype(BF16)
        slot = line_buf.at[n, s]
        flying[key] = [send(slot, slot, step_peer(d)) for d in order]

    def land(key):
        n, j = keys.index(key), key[1]
        for copy in flying[key]:
            copy.wait_recv()
        total = local_eps[key]
        for i in range(S):
            total = total + line_buf[n, i].astype(F32)
        drift[key] = keeps[j] * state[key] + coefs[j] * total

    for act, key in PLAN:
        {"launch": launch, "relay": relay, "land": land}[act](key)

    old = [start] * S
    norms_out = []
    for it in range(ITERS):
        new, run = [], start
        for j in range(S):
            new.append(run)
            if j < S - 1:
                run = run + drift[(min(it, j), j)]
        square = jnp.zeros((1, 1), F32)
        for j in range(S):
            change = new[j] - old[j]
            square = square + jnp.sum(
                jnp.sum(change * change, axis=0, keepdims=True), axis=1, keepdims=True
            )
        norms_out.append(jnp.sqrt(square / (S * C * N) + 1e-06))
        old = new
    lane = lax.broadcasted_iota(jnp.int32, res_ref.shape, 1)
    res = jnp.zeros(res_ref.shape, F32)
    for it in range(ITERS):
        res = jnp.where(lane == it, norms_out[it], res)
    res_ref[...] = res
    mine = jnp.zeros((C, N), F32)
    for j in range(S):
        mine = jnp.where(s == j, old[j] + drift[(min(ITERS - 1, j), j)], mine)
    half = mine[:, 0:rows]
    for i in range(1, F):
        half = jnp.where(f == i, mine[:, i * rows : (i + 1) * rows], half)
    traj_ref[0] = half
    for copy in started:
        copy.wait_send()


PLAN = (
    ("launch", (0, 0)),
    ("launch", (0, 1)),
    ("relay", (0, 0)),
    ("launch", (0, 2)),
    ("relay", (0, 1)),
    ("land", (0, 0)),
    ("launch", (1, 1)),
    ("relay", (0, 2)),
    ("relay", (1, 1)),
    ("land", (0, 1)),
    ("launch", (1, 2)),
    ("land", (1, 1)),
    ("launch", (2, 2)),
    ("relay", (1, 2)),
    ("relay", (2, 2)),
    ("land", (0, 2)),
    ("land", (1, 2)),
    ("land", (2, 2)),
    ("launch", (3, 3)),
    ("relay", (3, 3)),
    ("land", (3, 3)),
)


def local_heads(
    start_noise,
    position,
    time_table,
    time_index,
    sched_index,
    coef_keep,
    coef_noise,
    w_in,
    norm_gain,
    w_qkv,
    w_proj,
    w_final,
):
    S, F, H = (lax.axis_size(a) for a in ("step", "frame", "head"))
    R = w_qkv.shape[0]
    C, rows = start_noise.shape
    D = position.shape[1]
    N = rows * F
    PL = F * H
    pad = -(-3 * HDIM // 128) * 128
    n_evals = len(evals_of(S))
    n_sems = 3 * (S - 1) + 2 * (F - 1) + n_evals * (PL - 1 + S - 1)
    vmem = pl.BlockSpec(memory_space=pltpu.VMEM)
    smem = pl.BlockSpec(memory_space=pltpu.SMEM)
    here = pl.BlockSpec(memory_space=pl.ANY)
    traj, res = pl.pallas_call(
        functools.partial(kernel, S, F, H),
        out_shape=(
            jax.ShapeDtypeStruct((1, C, rows), F32),
            jax.ShapeDtypeStruct((1, ITERS), F32),
        ),
        in_specs=[here, here, here, smem, smem] + [here] * 7,
        out_specs=(vmem, vmem),
        scratch_shapes=[
            pltpu.VMEM(time_table.shape, BF16),
            pltpu.VMEM((1, coef_keep.shape[0]), F32),
            pltpu.VMEM((1, coef_noise.shape[0]), F32),
            pltpu.VMEM(w_in.shape, BF16),
            pltpu.VMEM((1, D), F32),
            pltpu.VMEM((3, R, w_qkv.shape[2]), BF16),
            pltpu.VMEM(w_proj.shape, BF16),
            pltpu.VMEM(w_final.shape, BF16),
            pltpu.VMEM((S, R, pad), BF16),
            pltpu.VMEM((S, C, HDIM), F32),
            pltpu.VMEM((F, rows, D), BF16),
            pltpu.VMEM((F, C, rows), F32),
            pltpu.VMEM((S, 8, time_table.shape[0]), F32),
            pltpu.VMEM((S, 2 * HDIM + 3 * C, N), F32),
            pltpu.VMEM((n_evals, PL, C, N), BF16),
            pltpu.VMEM((n_evals, S, C, N), BF16),
            pltpu.VMEM((S, R, pad), BF16),
            pltpu.VMEM((S, C, HDIM), F32),
            pltpu.SemaphoreType.DMA((n_sems + 10,)),
            pltpu.SemaphoreType.DMA((n_sems,)),
        ],
        compiler_params=pltpu.CompilerParams(
            collective_id=0, has_side_effects=True, vmem_limit_bytes=60 * 1024 * 1024
        ),
    )(
        start_noise,
        position,
        time_table,
        time_index,
        sched_index,
        coef_keep[None],
        coef_noise[None],
        w_in,
        norm_gain[None],
        jnp.transpose(w_qkv, (1, 0, 2)),
        w_proj,
        w_final,
    )
    return traj, res.reshape(ITERS)


def one_head_each(mesh, start_noise, time_index, w_qkv, time_table):
    S, F, H = (mesh.shape[a] for a in ("step", "frame", "head"))
    return (
        S == ITERS
        and time_index.shape[0] == S
        and w_qkv.shape[2] == S * F * H * HDIM
        and w_qkv.shape[0] % (16 * S) == 0
        and start_noise.shape[1] % (128 * F) == 0
        and start_noise.shape[1] // F <= time_table.shape[0]
        and time_table.shape[0] % 128 == 0
    )


def solution(mesh):
    def call(*args):
        fits = one_head_each(mesh, args[0], args[3], args[9], args[2])
        return jax.shard_map(
            local_heads if fits else local_any,
            mesh=mesh,
            in_specs=(
                P("parts", "frame"),
                P("frame", None),
                P(),
                P("step"),
                P("step"),
                P(),
                P(),
                P(),
                P(),
                P("step", None, "head"),
                P("step", "head"),
                P(),
            ),
            out_specs=(P("step", "parts", "frame"), P("parts")),
            check_vma=False,
        )(*args)

    return call
```

```python
import functools
import math

import jax
import jax.numpy as jnp
from jax import lax
from jax.experimental import pallas as pl
from jax.experimental.pallas import tpu as pltpu
from jax.sharding import PartitionSpec as P

HDIM = 72
ITERS = 4


def entering(value, axis, combine, identity):
    count, here = (lax.axis_size(axis), lax.axis_index(axis))
    everything = lax.all_gather(value, axis)
    start = jnp.broadcast_to(jnp.asarray(identity, value.dtype), value.shape)

    def hop(k, before):
        reached = k < here
        new = combine(before, everything[k])
        return jnp.where(reached, new, before)

    return lax.fori_loop(0, count, hop, start)


def add_terms(first, second):
    return first + second


def local_any(
    start_noise,
    position,
    time_table,
    time_index,
    sched_index,
    coef_keep,
    coef_noise,
    w_in,
    norm_gain,
    w_qkv,
    w_proj,
    w_final,
):
    w_qkv_all, w_proj_all = (
        lax.all_gather(w_qkv, "step", axis=0, tiled=True),
        lax.all_gather(w_proj, "step", axis=0, tiled=True),
    )
    batch_steps = time_index.shape[0]
    row_count = start_noise.shape[1]
    table_rows = time_table.shape[0]
    pick_time = (time_index[:, None] == jnp.arange(table_rows)[None, :]).astype(jnp.bfloat16)
    time_embed = jnp.dot(pick_time, time_table, preferred_element_type=jnp.float32)
    pick_sched = (sched_index[:, None] == jnp.arange(table_rows)[None, :]).astype(jnp.float32)
    keep_rate = jnp.sum(pick_sched * coef_keep[None, :], axis=1)
    noise_rate = jnp.sum(pick_sched * coef_noise[None, :], axis=1)
    heads_local = w_qkv_all.shape[2] // HDIM
    cell_count = (
        batch_steps
        * lax.axis_size("step")
        * start_noise.shape[0]
        * row_count
        * lax.axis_size("frame")
    )
    states = start_noise[None]
    drift_term = jnp.zeros_like(states)
    residual_list = []
    for iteration in range(ITERS):
        latent_bf = states.astype(jnp.bfloat16)
        hidden = (
            jnp.einsum("bcr,cd->brd", latent_bf, w_in, preferred_element_type=jnp.float32)
            + position
            + time_embed[:, None, :]
        )
        normed = (
            hidden * lax.rsqrt(jnp.mean(hidden * hidden, axis=2, keepdims=True) + 1e-06) * norm_gain
        ).astype(jnp.bfloat16)
        projected = jnp.einsum(
            "brd,dkq->brkq", normed, w_qkv_all, preferred_element_type=jnp.float32
        ).astype(jnp.bfloat16)
        queries = projected[:, :, 0].reshape(batch_steps, row_count, heads_local, HDIM)
        score_scale = 1.0 / math.sqrt(HDIM)
        keys_values = projected[:, :, 1:3]
        piece = lax.all_gather(keys_values, "frame", axis=1, tiled=True)
        top_old = jnp.full((batch_steps, heads_local, row_count), -1e30, jnp.float32)
        piece_rows = piece.shape[1]
        keys_blk = piece[:, :, 0].reshape(batch_steps, piece_rows, heads_local, HDIM)
        values_blk = piece[:, :, 1].reshape(batch_steps, piece_rows, heads_local, HDIM)
        scores = (
            jnp.einsum("bqhe,bkhe->bhqk", queries, keys_blk, preferred_element_type=jnp.float32)
            * score_scale
        )
        top_new = jnp.maximum(top_old, jnp.max(scores, axis=3))
        weights_exp = jnp.exp(scores - top_new[:, :, :, None])
        total_new = jnp.sum(weights_exp, axis=3)
        update = jnp.einsum(
            "bhqk,bkhe->bqhe",
            weights_exp.astype(jnp.bfloat16),
            values_blk,
            preferred_element_type=jnp.float32,
        )
        accum = update
        top_final, total_final, accum = (top_new, total_new, accum)
        attended = accum / jnp.transpose(total_final, (0, 2, 1))[:, :, :, None]
        attn_mixed = attended.reshape(batch_steps, row_count, heads_local * HDIM).astype(
            jnp.bfloat16
        )
        partial_value = jnp.einsum(
            "brq,dq->brd", attn_mixed, w_proj_all, preferred_element_type=jnp.float32
        )
        head_total = lax.psum(partial_value, "head")
        joined = (hidden + head_total).astype(jnp.bfloat16)
        predicted = jnp.einsum("cd,brd->bcr", w_final, joined, preferred_element_type=jnp.float32)
        drift_term = keep_rate[:, None, None] * states + noise_rate[:, None, None] * predicted
        local_incl = jnp.cumsum(drift_term, axis=0)
        local_total = local_incl[-1]
        earlier = entering(local_total, "step", add_terms, jnp.zeros_like(local_total))
        before = earlier[None] + (local_incl - drift_term)
        new_states = start_noise[None] + before
        change = new_states - states
        square_sum = jnp.sum(change * change)
        summed = lax.psum(square_sum, ("step", "frame"))
        residual_list.append(jnp.sqrt(summed / cell_count + 1e-06))
        states = new_states
    residual_norms = jnp.stack(residual_list)
    trajectory = states + drift_term
    return (trajectory, residual_norms)


MESH = pl.DeviceIdType.MESH
F32 = jnp.float32
BF16 = jnp.bfloat16


def dot(a, b, ca=1, cb=0):
    return lax.dot_general(a, b, (((ca,), (cb,)), ((), ())), preferred_element_type=F32)


def dot_exact(a, b):
    return lax.dot_general(
        a, b, (((1,), (0,)), ((), ())), precision=lax.Precision.HIGHEST, preferred_element_type=F32
    )


def two(a):
    high = a.astype(BF16)
    return high, (a - high.astype(F32)).astype(BF16)


def evals_of(steps):
    return [(i, j) for j in range(steps - 1) for i in range(min(j, ITERS - 1) + 1)] + [
        (min(ITERS, steps) - 1, steps - 1)
    ]


def kernel(
    S,
    F,
    H,
    noise_hbm,
    pos_hbm,
    table_hbm,
    tidx_ref,
    sidx_ref,
    keep_hbm,
    coef_hbm,
    win_hbm,
    gain_hbm,
    wqkv_hbm,
    wproj_hbm,
    wfin_hbm,
    traj_ref,
    res_ref,
    table_ref,
    keep_ref,
    coef_ref,
    win_ref,
    gain_ref,
    wqkv_ref,
    wproj_ref,
    wfin_ref,
    w_buf,
    m_buf,
    pos_buf,
    noise_buf,
    meta_buf,
    base_buf,
    plane_buf,
    line_buf,
    wsend_ref,
    msend_ref,
    ssem,
    rsem,
):
    s, f, h = (lax.axis_index(a) for a in ("step", "frame", "head"))
    loads = [
        pltpu.make_async_copy(src, dst, ssem.at[ssem.shape[0] - 1 - n])
        for n, (src, dst) in enumerate(
            (
                (pos_hbm, pos_buf.at[f]),
                (noise_hbm, noise_buf.at[f]),
                (keep_hbm, keep_ref),
                (coef_hbm, coef_ref),
                (wqkv_hbm, wqkv_ref),
                (wproj_hbm, wproj_ref),
                (wfin_hbm, wfin_ref),
                (table_hbm, table_ref),
                (win_hbm, win_ref),
                (gain_hbm, gain_ref),
            )
        )
    ]
    for copy in loads:
        copy.start()
    PL = F * H
    q_me = f * H + h
    C, rows = noise_buf.shape[1:]
    D = pos_buf.shape[2]
    N = rows * F
    pad = w_buf.shape[2]
    lanes = table_ref.shape[0]

    def step_peer(d):
        return {"step": lax.rem(s + d, S)}

    def plane_peer(d):
        t = lax.rem(q_me + d, PL)
        return {"frame": t // H, "head": lax.rem(t, H)}

    def frame_peer(d):
        return {"frame": lax.rem(f + d, F)}

    Y, y = lax.axis_size("parts"), lax.axis_index("parts")

    def part_peer(d):
        return {"parts": lax.rem(y + d, Y)}

    barrier = pltpu.get_barrier_semaphore()
    for d in range(1, Y):
        pl.semaphore_signal(barrier, inc=1, device_id=part_peer(d), device_id_type=MESH)
    for d in range(1, S):
        pl.semaphore_signal(barrier, inc=1, device_id=step_peer(d), device_id_type=MESH)
    for d in range(1, PL):
        pl.semaphore_signal(barrier, inc=1, device_id=plane_peer(d), device_id_type=MESH)

    for copy in loads[:4]:
        copy.wait()
    row_id = lax.broadcasted_iota(jnp.int32, (8, lanes), 0)
    lane_id = lax.broadcasted_iota(jnp.int32, (1, lanes), 1)
    hot_t = jnp.where(lane_id == tidx_ref[0], 1.0, 0.0)
    hot_s = lane_id == sidx_ref[0]
    keep = jnp.sum(jnp.where(hot_s, keep_ref[...], 0.0), axis=1, keepdims=True)
    coef = jnp.sum(jnp.where(hot_s, coef_ref[...], 0.0), axis=1, keepdims=True)
    meta_buf[s] = jnp.where(row_id == 0, hot_t, jnp.where(row_id == 1, keep, coef))
    pl.semaphore_wait(barrier, S - 1 + PL - 1 + Y - 1)

    count = [0]
    started = []

    def send(src, dst, peer):
        k = count[0]
        count[0] += 1
        copy = pltpu.make_async_remote_copy(
            src_ref=src,
            dst_ref=dst,
            send_sem=ssem.at[k],
            recv_sem=rsem.at[k],
            device_id=peer,
            device_id_type=MESH,
        )
        copy.start()
        started.append(copy)
        return copy

    order = sorted(range(1, S), key=lambda d: abs(d - S / 2))
    early = [send(meta_buf.at[s], meta_buf.at[s], step_peer(d)) for d in order]
    early += [send(noise_buf.at[f], noise_buf.at[f], frame_peer(d)) for d in range(1, F)]
    early += [send(pos_buf.at[f], pos_buf.at[f], frame_peer(d)) for d in range(1, F)]
    for copy in loads[4:7]:
        copy.wait()
    R = wqkv_ref.shape[1]
    for i in range(F):

        @pl.when(f == i)
        def _():
            for t in range(S):
                low = (t * F + i) * HDIM
                parts = [wqkv_ref[p, :, low : low + HDIM] for p in range(3)]
                parts.append(jnp.zeros((R, pad - 3 * HDIM), BF16))
                wsend_ref[t] = jnp.concatenate(parts, axis=1)

    share = pl.ds(pl.multiple_of(y * (R // Y), 16), R // Y)
    shares = [
        send(wsend_ref.at[lax.rem(s + d, S), share], w_buf.at[s, share], step_peer(d))
        for d in order
    ]
    late = []
    rows_of = wfin_ref[:, 0:R].astype(F32)
    for j in range(1, S):
        rows_of = jnp.where(s == j, wfin_ref[:, j * R : (j + 1) * R].astype(F32), rows_of)
    folded = dot(rows_of.astype(BF16), wproj_ref[...])
    for t in range(S):
        picked = folded[:, t * F * HDIM : (t * F + 1) * HDIM]
        for i in range(1, F):
            low = (t * F + i) * HDIM
            picked = jnp.where(f == i, folded[:, low : low + HDIM], picked)
        msend_ref[t] = picked
    late += [
        send(msend_ref.at[lax.rem(s + d, S)], m_buf.at[s], step_peer(d)) for d in order
    ]
    w_buf[s] = wsend_ref[s]
    m_buf[s] = msend_ref[s]
    for copy in loads[7:]:
        copy.wait()
    for copy in early:
        copy.wait_recv()

    pos = pos_buf[...].reshape(N, D)
    start = jnp.concatenate([noise_buf[i] for i in range(F)], axis=1)
    metas = [meta_buf[j] for j in range(S)]
    hot = jnp.concatenate(
        [m[0:1] for m in metas] + [jnp.zeros((8 - S, lanes), F32)], axis=0
    ).astype(BF16)
    keeps = [jnp.concatenate([m[1:2, :rows]] * F, axis=1) for m in metas]
    coefs = [jnp.concatenate([m[2:3, :rows]] * F, axis=1) for m in metas]
    temb = dot(hot, table_ref[...])
    temb_b = temb.astype(BF16)
    gain = gain_ref[...]
    w_in = win_ref[...]
    posf = pos.astype(F32)
    p_hi, p_lo = two(posf * gain)
    side = jnp.concatenate(
        [w_in.astype(F32), temb, jnp.zeros((128 - C - 8, D), F32)], axis=0
    )
    q_hi, q_lo = two(side * gain)
    left = jnp.concatenate([p_hi, p_lo, q_hi, q_lo], axis=0)
    ends = jnp.concatenate([w_in, wfin_ref[...]], axis=0)
    ends_pos = dot(ends, pos, 1, 1)
    ends_t = dot(ends, temb_b, 1, 1)
    ends_in = dot(ends, w_in, 1, 1)
    sq_hi, sq_lo = two(posf * posf)
    ones = jnp.ones((8, D), BF16)
    norm_p = dot(ones, sq_hi, 1, 1) + dot(ones, sq_lo, 1, 1)
    cross = dot(temb_b, pos, 1, 1)
    norm_t = jnp.sum(temb * temb, axis=1, keepdims=True)
    norms = [norm_p[0:1] + 2.0 * cross[j : j + 1] + norm_t[j : j + 1] for j in range(S)]

    for d, copy in zip(order, shares):
        copy.wait_recv()
        slot = w_buf.at[lax.rem(s + S - d, S), share]
        late += [send(slot, slot, part_peer(e)) for e in range(1, Y)]
    for copy in late:
        copy.wait_recv()

    wide = dot(left, w_buf[...].reshape(D, pad))
    by_pos = jnp.transpose(wide[0:N] + wide[N : 2 * N])
    by_side = jnp.transpose(wide[2 * N : 2 * N + 128] + wide[2 * N + 128 :])
    mix = m_buf[0]
    for j in range(1, S):
        mix = mix + m_buf[j]
    scale = 1.4426950408889634 / math.sqrt(HDIM)

    def table_of(t):
        return jnp.concatenate(
            [
                t[0:HDIM] * scale,
                t[HDIM : 2 * HDIM],
                dot_exact(mix, t[2 * HDIM : 3 * HDIM]),
            ],
            axis=0,
        )

    tab_pos, tab_side = table_of(by_pos), table_of(by_side)
    big_hi, big_lo = two(jnp.concatenate([tab_side[:, 0:C], ends_in], axis=0))
    for j in range(S):
        base_buf[j] = jnp.concatenate(
            [
                tab_pos + tab_side[:, C + j : C + j + 1],
                2.0 * (ends_pos[0:C] + ends_t[0:C, j : j + 1]),
                ends_pos[C : 2 * C] + ends_t[C : 2 * C, j : j + 1],
            ],
            axis=0,
        )
    QK = 2 * HDIM

    def partial(x, j):
        xb = x.astype(BF16)
        lin = dot(big_hi, xb) + dot(big_lo, xb) + base_buf[j]
        square = jnp.sum(xb.astype(F32) * lin[QK + C : QK + 2 * C], axis=0, keepdims=True)
        square = jnp.maximum(square + norms[j], 0.0)
        r = lax.rsqrt(square * (1.0 / D) + 1e-06)
        q = (lin[0:HDIM] * r).astype(BF16)
        k = (lin[HDIM:QK] * r).astype(BF16)
        v_hi, v_lo = two(lin[QK : QK + C] * r)
        scores = dot(k, q, 0, 0)
        e = jnp.exp2(scores - jnp.max(scores, axis=0, keepdims=True)).astype(BF16)
        o = dot(jnp.concatenate([v_hi, v_lo, jnp.ones((C, N), BF16)], axis=0), e)
        out = (o[0:C] + o[C : 2 * C]) / o[2 * C : 2 * C + 1]
        return out, lin[QK + 2 * C : QK + 3 * C]

    keys = evals_of(S)
    state, local_eps, drift, flying = {}, {}, {}, {}

    def launch(key):
        i, j = key
        n = keys.index(key)
        x = start
        for m in range(j if i else 0):
            x = x + drift[(min(i - 1, m), m)]
        state[key] = x
        part, local_eps[key] = partial(x, j)
        plane_buf[n, q_me] = part.astype(BF16)
        slot = plane_buf.at[n, q_me]
        flying[key] = [send(slot, slot, plane_peer(d)) for d in range(1, PL)]

    def relay(key):
        n = keys.index(key)
        for copy in flying[key]:
            copy.wait_recv()
        total = plane_buf[n, 0].astype(F32)
        for i in range(1, PL):
            total = total + plane_buf[n, i].astype(F32)
        line_buf[n, s] = total.astype(BF16)
        slot = line_buf.at[n, s]
        flying[key] = [send(slot, slot, step_peer(d)) for d in order]

    def land(key):
        n, j = keys.index(key), key[1]
        for copy in flying[key]:
            copy.wait_recv()
        total = local_eps[key]
        for i in range(S):
            total = total + line_buf[n, i].astype(F32)
        drift[key] = keeps[j] * state[key] + coefs[j] * total

    for act, key in PLAN:
        {"launch": launch, "relay": relay, "land": land}[act](key)

    old = [start] * S
    norms_out = []
    for it in range(ITERS):
        new, run = [], start
        for j in range(S):
            new.append(run)
            if j < S - 1:
                run = run + drift[(min(it, j), j)]
        square = jnp.zeros((1, 1), F32)
        for j in range(S):
            change = new[j] - old[j]
            square = square + jnp.sum(
                jnp.sum(change * change, axis=0, keepdims=True), axis=1, keepdims=True
            )
        norms_out.append(jnp.sqrt(square / (S * C * N) + 1e-06))
        old = new
    lane = lax.broadcasted_iota(jnp.int32, res_ref.shape, 1)
    res = jnp.zeros(res_ref.shape, F32)
    for it in range(ITERS):
        res = jnp.where(lane == it, norms_out[it], res)
    res_ref[...] = res
    mine = jnp.zeros((C, N), F32)
    for j in range(S):
        mine = jnp.where(s == j, old[j] + drift[(min(ITERS - 1, j), j)], mine)
    half = mine[:, 0:rows]
    for i in range(1, F):
        half = jnp.where(f == i, mine[:, i * rows : (i + 1) * rows], half)
    traj_ref[0] = half
    for copy in started:
        copy.wait_send()


PLAN = (
    ("launch", (0, 0)),
    ("launch", (0, 1)),
    ("relay", (0, 0)),
    ("launch", (0, 2)),
    ("relay", (0, 1)),
    ("land", (0, 0)),
    ("launch", (1, 1)),
    ("relay", (0, 2)),
    ("relay", (1, 1)),
    ("land", (0, 1)),
    ("launch", (1, 2)),
    ("land", (1, 1)),
    ("launch", (2, 2)),
    ("relay", (1, 2)),
    ("relay", (2, 2)),
    ("land", (0, 2)),
    ("land", (1, 2)),
    ("land", (2, 2)),
    ("launch", (3, 3)),
    ("relay", (3, 3)),
    ("land", (3, 3)),
)


def local_heads(
    start_noise,
    position,
    time_table,
    time_index,
    sched_index,
    coef_keep,
    coef_noise,
    w_in,
    norm_gain,
    w_qkv,
    w_proj,
    w_final,
):
    S, F, H = (lax.axis_size(a) for a in ("step", "frame", "head"))
    R = w_qkv.shape[0]
    C, rows = start_noise.shape
    D = position.shape[1]
    N = rows * F
    PL = F * H
    pad = -(-3 * HDIM // 128) * 128
    n_evals = len(evals_of(S))
    n_sems = (2 + lax.axis_size("parts")) * (S - 1) + 2 * (F - 1) + n_evals * (PL - 1 + S - 1)
    vmem = pl.BlockSpec(memory_space=pltpu.VMEM)
    smem = pl.BlockSpec(memory_space=pltpu.SMEM)
    here = pl.BlockSpec(memory_space=pl.ANY)
    traj, res = pl.pallas_call(
        functools.partial(kernel, S, F, H),
        out_shape=(
            jax.ShapeDtypeStruct((1, C, rows), F32),
            jax.ShapeDtypeStruct((1, ITERS), F32),
        ),
        in_specs=[here, here, here, smem, smem] + [here] * 7,
        out_specs=(vmem, vmem),
        scratch_shapes=[
            pltpu.VMEM(time_table.shape, BF16),
            pltpu.VMEM((1, coef_keep.shape[0]), F32),
            pltpu.VMEM((1, coef_noise.shape[0]), F32),
            pltpu.VMEM(w_in.shape, BF16),
            pltpu.VMEM((1, D), F32),
            pltpu.VMEM((3, R, w_qkv.shape[2]), BF16),
            pltpu.VMEM(w_proj.shape, BF16),
            pltpu.VMEM(w_final.shape, BF16),
            pltpu.VMEM((S, R, pad), BF16),
            pltpu.VMEM((S, C, HDIM), F32),
            pltpu.VMEM((F, rows, D), BF16),
            pltpu.VMEM((F, C, rows), F32),
            pltpu.VMEM((S, 8, time_table.shape[0]), F32),
            pltpu.VMEM((S, 2 * HDIM + 3 * C, N), F32),
            pltpu.VMEM((n_evals, PL, C, N), BF16),
            pltpu.VMEM((n_evals, S, C, N), BF16),
            pltpu.VMEM((S, R, pad), BF16),
            pltpu.VMEM((S, C, HDIM), F32),
            pltpu.SemaphoreType.DMA((n_sems + 10,)),
            pltpu.SemaphoreType.DMA((n_sems,)),
        ],
        compiler_params=pltpu.CompilerParams(
            collective_id=0, has_side_effects=True, vmem_limit_bytes=60 * 1024 * 1024
        ),
    )(
        start_noise,
        position,
        time_table,
        time_index,
        sched_index,
        coef_keep[None],
        coef_noise[None],
        w_in,
        norm_gain[None],
        jnp.transpose(w_qkv, (1, 0, 2)),
        w_proj,
        w_final,
    )
    return traj, res.reshape(ITERS)


def one_head_each(mesh, start_noise, time_index, w_qkv, time_table):
    S, F, H = (mesh.shape[a] for a in ("step", "frame", "head"))
    return (
        S == ITERS
        and time_index.shape[0] == S
        and w_qkv.shape[2] == S * F * H * HDIM
        and w_qkv.shape[0] % (16 * S * mesh.shape["parts"]) == 0
        and start_noise.shape[1] % (128 * F) == 0
        and start_noise.shape[1] // F <= time_table.shape[0]
        and time_table.shape[0] % 128 == 0
    )


def solution(mesh):
    def call(*args):
        fits = one_head_each(mesh, args[0], args[3], args[9], args[2])
        return jax.shard_map(
            local_heads if fits else local_any,
            mesh=mesh,
            in_specs=(
                P("parts", "frame"),
                P("frame", None),
                P(),
                P("step"),
                P("step"),
                P(),
                P(),
                P(),
                P(),
                P("step", None, "head"),
                P("step", "head"),
                P(),
            ),
            out_specs=(P("step", "parts", "frame"), P("parts")),
            check_vma=False,
        )(*args)

    return call
```
